32 devices in a mesh: rep: 8 (over y, x, core), shard: 4 (over z).
Axes of the slice: x: 2, y: 2, z: 4, core: 2. Of those that a mesh axis runs over, the one named last changes fastest.
Arguments:
- tokens: bfloat16 [25216, 384], P(('rep', 'shard')), may hold values from -8 to 8
- cotangent: bfloat16 [25216, 384], P(('rep', 'shard')), may hold values from -6 to 6
- ln1_gain: bfloat16 [384], P('shard'), may hold values from 0.5 to 1.5
- ln1_bias: bfloat16 [384], P('shard'), may hold values from -3 to 3
- w_qkv: bfloat16 [384, 1152], P('shard'), may hold values from -1 to 1
- bias_qv: bfloat16 [2, 384], P(None, 'shard'), may hold values from -3 to 3
- w_out: bfloat16 [384, 384], P('shard'), may hold values from -0.875 to 0.875
- bias_out: bfloat16 [384], P('shard'), may hold values from -3 to 3
- ln2_gain: bfloat16 [384], P('shard'), may hold values from 0.5 to 1.5
- ln2_bias: bfloat16 [384], P('shard'), may hold values from -3 to 3
- w_fc1: bfloat16 [384, 1536], P('shard'), may hold values from -0.3125 to 0.3125
- bias_fc1: bfloat16 [1536], P('shard'), may hold values from -3 to 3
- w_fc2: bfloat16 [1536, 384], P('shard'), may hold values from -0.15625 to 0.15625
- bias_fc2: bfloat16 [384], P('shard'), may hold values from -3 to 3
Outputs:
- layer_out: bfloat16 [25216, 384], P(('rep', 'shard'))
- grad_tokens: bfloat16 [25216, 384], P(('rep', 'shard'))
- grad_ln1_gain: float32 [384], P('shard')
- grad_ln1_bias: float32 [384], P('shard')
- grad_w_qkv: float32 [384, 1152], P('shard')
- grad_bias_qv: float32 [2, 384], P(None, 'shard')
- grad_w_out: float32 [384, 384], P('shard')
- grad_bias_out: float32 [384], P('shard')
- grad_ln2_gain: float32 [384], P('shard')
- grad_ln2_bias: float32 [384], P('shard')
- grad_w_fc1: float32 [384, 1536], P('shard')
- grad_bias_fc1: float32 [1536], P('shard')
- grad_w_fc2: float32 [1536, 384], P('shard')
- grad_bias_fc2: float32 [384], P('shard')
The draws below stay inside these ranges and needn't reach their ends.
All inputs are finite; a program needn't handle non-finite values.
Results may differ from the reference program's by a relative error of at most 0.015.
The reference program's roundings to bfloat16 on the way (of `hidden_one`, `mixed`, `hidden_two`, `act_b`, `grad_mixed` and `grad_scores`) count: a program that leaves them out, or rounds other values in their place, can miss the bound.
Values may be sent and summed in bfloat16 or wider, within the bound.
A program may use at most 128 MiB of HBM per device.

```python
import jax
import jax.numpy as jnp
from jax import lax

D = 384
HEADS = 6
HEAD_DIM = 64
FF = 1536
SEQ = 197
TOKENS = 25216


def draw_tokens(key, part):
    values = jax.random.truncated_normal(jax.random.fold_in(key, 11), -6.0, 6.0, (TOKENS, D), jnp.float32)
    return values.astype(jnp.bfloat16)


def draw_w_qkv(key, part):
    values = jax.random.truncated_normal(jax.random.fold_in(key, 12), -6.0, 6.0, (D, 3 * D), jnp.float32) * float(D) ** (-0.5)
    return values.astype(jnp.bfloat16)


def block_levels(key, dims, shards, smallest, largest):
    def one(dim, blocks):
        heights = jax.random.uniform(jax.random.fold_in(jax.random.fold_in(key, 6), dim), (blocks,), jnp.float32, smallest / len(shards), largest / len(shards))
        return jnp.repeat(jnp.exp(heights), dims[dim] // blocks).reshape((-1,) + (1,) * (len(dims) - dim - 1))

    factor_of = one(*shards[0])
    for cut in shards[1:]:
        factor_of = factor_of * one(*cut)
    return factor_of


def scatter_about(key, dims, scale, limit, cuts=(), held_as=jnp.bfloat16):
    level = block_levels(key, dims, cuts, -0.22, 0.18) if cuts else 1.0
    array = jax.random.normal(key, dims, jnp.float32) * scale * level
    return jnp.minimum(jnp.maximum(array, -limit), limit).astype(held_as)


def setup_inputs(seed: int = 0) -> dict:
    key_list = jax.random.split(jax.random.key(seed), 15)
    tokens = draw_tokens(jax.random.fold_in(key_list[14], 71), 0)
    cotangent = scatter_about(key_list[1], (TOKENS, D), 1.0, 6.0, ((0, 32),))
    ln1_gain = jnp.clip(1.0 + 0.1 * jax.random.normal(key_list[2], (D,), jnp.float32), 0.5, 1.5).astype(jnp.bfloat16)
    ln1_bias = scatter_about(key_list[3], (D,), 0.3, 3.0, ((0, 4),))
    w_qkv = draw_w_qkv(jax.random.fold_in(key_list[14], 71), 0)
    bias_qv = scatter_about(key_list[5], (2, D), 0.5, 3.0, ((1, 4),))
    w_out = scatter_about(key_list[6], (D, D), (D // 8) ** -0.5, 0.875, ((0, 4),))
    bias_out = scatter_about(key_list[7], (D,), 0.5, 3.0, ((0, 4),))
    ln2_gain = jnp.clip(1.0 + 0.1 * jax.random.normal(key_list[8], (D,), jnp.float32), 0.5, 1.5).astype(jnp.bfloat16)
    ln2_bias = scatter_about(key_list[9], (D,), 0.3, 3.0, ((0, 4),))
    w_fc1 = scatter_about(key_list[10], (D, FF), D ** -0.5, 0.3125, ((0, 4),))
    bias_fc1 = scatter_about(key_list[11], (FF,), 0.5, 3.0, ((0, 4),))
    w_fc2 = scatter_about(key_list[12], (FF, D), FF ** -0.5, 0.15625, ((0, 4),))
    bias_fc2 = scatter_about(key_list[13], (D,), 0.5, 3.0, ((0, 4),))
    return dict(tokens=tokens, cotangent=cotangent, ln1_gain=ln1_gain, ln1_bias=ln1_bias, w_qkv=w_qkv, bias_qv=bias_qv, w_out=w_out, bias_out=bias_out, ln2_gain=ln2_gain, ln2_bias=ln2_bias, w_fc1=w_fc1, bias_fc1=bias_fc1, w_fc2=w_fc2, bias_fc2=bias_fc2)


inverse_root_two = 0.7071067811865476
inverse_root_tau = 0.3989422804014327

def norm_forward(values, gain, shift):
    centre = lax.optimization_barrier(jnp.mean(values, axis=-1, keepdims=True))
    centred = values - centre
    inv_std = lax.rsqrt(lax.optimization_barrier(jnp.mean(centred * centred, axis=-1, keepdims=True)) + 1e-06)
    normed = centred * inv_std
    return (normed * gain + shift, normed, inv_std)

def norm_backward(grad_out, normed, inv_std, gain):
    scaled = grad_out * gain
    grad_in = inv_std * (scaled - lax.optimization_barrier(jnp.mean(scaled, axis=-1, keepdims=True)) - normed * lax.optimization_barrier(jnp.mean(scaled * normed, axis=-1, keepdims=True)))
    return (grad_in, lax.optimization_barrier(jnp.sum(grad_out * normed, axis=0)), lax.optimization_barrier(jnp.sum(grad_out, axis=0)))

def gelu_parts(values):
    normal_cdf = 0.5 * (1.0 + lax.erf(values * inverse_root_two))
    slope = normal_cdf + values * jnp.exp(-0.5 * values * values) * inverse_root_tau
    return (values * normal_cdf, slope)

def layer(tok_block, cot_block, gain_one, shift_one, qkv_weight, qv_shift, out_weight, out_shift, gain_two, shift_two, fc1_weight, fc1_shift, fc2_weight, fc2_shift):
    f32 = jnp.float32
    bf16 = jnp.bfloat16
    row_count = tok_block.shape[0]
    image_count = row_count // SEQ
    shape_four = (image_count, SEQ, HEADS, HEAD_DIM)
    score_scale = float(HEAD_DIM) ** (-0.5)
    x_float = tok_block.astype(f32)
    norm_one, normed_one, inv_one = norm_forward(x_float, gain_one, shift_one)
    hidden_one = norm_one.astype(bf16)
    projected = jnp.dot(hidden_one, qkv_weight, preferred_element_type=f32)
    query_rows = (projected[:, :D] + qv_shift[0]).astype(bf16)
    key_rows = projected[:, D:2 * D].astype(bf16)
    value_rows = (projected[:, 2 * D:] + qv_shift[1]).astype(bf16)
    query_four = query_rows.reshape(shape_four).astype(f32)
    key_four = key_rows.reshape(shape_four).astype(f32)
    value_four = value_rows.reshape(shape_four).astype(f32)
    scores = jnp.einsum('ishd,ithd->ihst', query_four, key_four) * score_scale
    row_max = lax.optimization_barrier(jnp.max(scores, axis=-1, keepdims=True))
    log_total = row_max + jnp.log(lax.optimization_barrier(jnp.sum(jnp.exp(scores - row_max), axis=-1, keepdims=True)))
    attn_probs = jnp.exp(scores - log_total)
    probs_b = attn_probs.astype(bf16).astype(f32)
    mixed = jnp.einsum('ihst,ithd->ishd', probs_b, value_four).reshape(row_count, D).astype(bf16)
    resid = x_float + jnp.dot(mixed, out_weight, preferred_element_type=f32) + out_shift
    norm_two, normed_two, inv_two = norm_forward(resid, gain_two, shift_two)
    hidden_two = norm_two.astype(bf16)
    pre_act = jnp.dot(hidden_two, fc1_weight, preferred_element_type=f32) + fc1_shift
    act_value, act_slope = gelu_parts(pre_act)
    act_b = act_value.astype(bf16)
    layer_out = (resid + jnp.dot(act_b, fc2_weight, preferred_element_type=f32) + fc2_shift).astype(bf16)
    cot_float = cot_block.astype(f32)
    grad_fc2 = jnp.dot(act_b.T, cot_block, preferred_element_type=f32)
    grad_fc2_shift = lax.optimization_barrier(jnp.sum(cot_float, axis=0))
    grad_pre = jnp.dot(cot_block, fc2_weight.T, preferred_element_type=f32) * act_slope
    grad_pre_b = grad_pre.astype(bf16)
    grad_fc1 = jnp.dot(hidden_two.T, grad_pre_b, preferred_element_type=f32)
    grad_fc1_shift = lax.optimization_barrier(jnp.sum(grad_pre, axis=0))
    grad_h2 = jnp.dot(grad_pre_b, fc1_weight.T, preferred_element_type=f32)
    grad_r2, grad_gain_two, grad_shift_two = norm_backward(grad_h2, normed_two, inv_two, gain_two)
    grad_resid = cot_float + grad_r2
    grad_resid_b = grad_resid.astype(bf16)
    grad_out_weight = jnp.dot(mixed.T, grad_resid_b, preferred_element_type=f32)
    grad_out_shift = lax.optimization_barrier(jnp.sum(grad_resid, axis=0))
    grad_mixed = jnp.dot(grad_resid_b, out_weight.T, preferred_element_type=f32).astype(bf16)
    grad_four = grad_mixed.reshape(shape_four).astype(f32)
    grad_values = jnp.einsum('ihst,ishd->ithd', probs_b, grad_four)
    grad_probs = jnp.einsum('ishd,ithd->ihst', grad_four, value_four)
    grad_scores = (attn_probs * (grad_probs - lax.optimization_barrier(jnp.sum(attn_probs * grad_probs, axis=-1, keepdims=True))) * score_scale).astype(bf16).astype(f32)
    grad_query = jnp.einsum('ihst,ithd->ishd', grad_scores, key_four).reshape(row_count, D)
    grad_keys = jnp.einsum('ihst,ishd->ithd', grad_scores, query_four).reshape(row_count, D)
    grad_values = grad_values.reshape(row_count, D)
    grad_qv_shift = jnp.stack([lax.optimization_barrier(jnp.sum(grad_query, axis=0)), lax.optimization_barrier(jnp.sum(grad_values, axis=0))])
    grad_qkv_b = jnp.concatenate([grad_query, grad_keys, grad_values], axis=1).astype(bf16)
    grad_qkv_weight = jnp.dot(hidden_one.T, grad_qkv_b, preferred_element_type=f32)
    grad_h1 = jnp.dot(grad_qkv_b, qkv_weight.T, preferred_element_type=f32)
    grad_r1, grad_gain_one, grad_shift_one = norm_backward(grad_h1, normed_one, inv_one, gain_one)
    grad_tok = (grad_resid + grad_r1).astype(bf16)
    grads = (grad_gain_one, grad_shift_one, grad_qkv_weight, grad_qv_shift, grad_out_weight, grad_out_shift, grad_gain_two, grad_shift_two, grad_fc1, grad_fc1_shift, grad_fc2, grad_fc2_shift)
    return (layer_out, grad_tok, grads)

def reference(tokens, cotangent, ln1_gain, ln1_bias, w_qkv, bias_qv, w_out, bias_out, ln2_gain, ln2_bias, w_fc1, bias_fc1, w_fc2, bias_fc2):
    f32 = jnp.float32
    params = (ln1_gain.astype(f32), ln1_bias.astype(f32), w_qkv, bias_qv.astype(f32), w_out, bias_out.astype(f32), ln2_gain.astype(f32), ln2_bias.astype(f32), w_fc1, bias_fc1.astype(f32), w_fc2, bias_fc2.astype(f32))
    block_rows = 16 * SEQ
    tok_blocks = tokens.reshape(-1, block_rows, D)
    cot_blocks = cotangent.reshape(-1, block_rows, D)
    shapes = (ln1_gain, ln1_bias, w_qkv, bias_qv, w_out, bias_out, ln2_gain, ln2_bias, w_fc1, bias_fc1, w_fc2, bias_fc2)
    start = tuple((jnp.zeros(item.shape, f32) for item in shapes))

    def advance(carry, blocks):
        layer_out, grad_tok, grads = layer(blocks[0], blocks[1], *params)
        return (jax.tree.map(lambda left, right: left + right, carry, grads), (layer_out, grad_tok))
    totals, (out_blocks, grad_blocks) = lax.scan(advance, start, (tok_blocks, cot_blocks))
    factor = float(TOKENS) ** (-0.5)
    scaled = tuple((item * factor for item in totals))
    return (out_blocks.reshape(TOKENS, D), grad_blocks.reshape(TOKENS, D), scaled[0], scaled[1], scaled[2], scaled[3], scaled[4], scaled[5], scaled[6], scaled[7], scaled[8], scaled[9], scaled[10], scaled[11])
```

```python
import functools

import jax
import jax.numpy as jnp
from jax import lax
from jax.experimental import pallas as pl
from jax.experimental.pallas import tpu as pltpu
from jax.sharding import PartitionSpec as P

HEADS = 6
HEAD_DIM = 64
SEQ = 197
VEC_ROWS = 16

F32 = jnp.float32
BF16 = jnp.bfloat16
inverse_root_two = 0.7071067811865476
inverse_root_tau = 0.3989422804014327


def bit_orders(bits):
    high = list(range(1, bits))
    return (high + [0], high[::-1] + [0])


def partners(bits, shards):
    me = lax.axis_index("rep")
    mine = [lax.rem(lax.div(me, 2**b), 2) for b in range(bits)]
    flipped = [me + (1 - 2 * mine[b]) * 2**b for b in range(bits)]
    z = lax.axis_index("shard")
    others = [lax.rem(z + d, shards) for d in range(shards)]
    return mine, flipped, z, others


def greet(bits, shards, flipped, others):
    barrier = pltpu.get_barrier_semaphore()
    for b in range(bits):
        pl.semaphore_signal(
            barrier, inc=1, device_id={"rep": flipped[b]}, device_id_type=pl.DeviceIdType.MESH
        )
    for d in range(1, shards):
        pl.semaphore_signal(
            barrier, inc=1, device_id={"shard": others[d]}, device_id_type=pl.DeviceIdType.MESH
        )
    pl.semaphore_wait(barrier, bits + shards - 1)


def remote(src, dst, send, recv, where):
    copy = pltpu.make_async_remote_copy(
        src_ref=src,
        dst_ref=dst,
        send_sem=send,
        recv_sem=recv,
        device_id=where,
        device_id_type=pl.DeviceIdType.MESH,
    )
    copy.start()
    return copy


def bit_index(bits, mine, free):
    return tuple(slice(None) if b in free else mine[b] for b in reversed(range(bits)))


def gather_kernel(bits, shards, own, full, local_sem, z_send, z_recv, send, recv):
    mine, flipped, z, others = partners(bits, shards)
    greet(bits, shards, flipped, others)
    piece = bit_index(bits, mine, ())
    hops = {}
    for d in range(1, shards):
        hops[d] = remote(
            own.at[piece], full.at[(z,) + piece], z_send.at[d], z_recv.at[d], {"shard": others[d]}
        )
    local = pltpu.make_async_copy(own, full.at[z], local_sem)
    local.start()
    orders = bit_orders(bits)
    copies = {}
    for t in range(bits):
        for d in range(1, shards):
            source = lax.rem(z - d + shards, shards)
            for half in range(2):
                if t == 0:
                    if half == 0:
                        hops[d].wait_recv()
                else:
                    copies[t - 1, d, half].wait_recv()
                bit = orders[half][t]
                where = (source,) + bit_index(bits, mine, orders[half][:t]) + (half,)
                copies[t, d, half] = remote(
                    full.at[where],
                    full.at[where],
                    send.at[t, d, half],
                    recv.at[t, d, half],
                    {"rep": flipped[bit]},
                )
    for d in range(1, shards):
        for half in range(2):
            copies[bits - 1, d, half].wait_recv()
    for copy in list(hops.values()) + list(copies.values()):
        copy.wait_send()
    local.wait()


def gather(packed, bits, shards):
    return pl.pallas_call(
        functools.partial(gather_kernel, bits, shards),
        out_shape=jax.ShapeDtypeStruct((shards,) + packed.shape, packed.dtype),
        in_specs=[pl.BlockSpec(memory_space=pltpu.VMEM)],
        out_specs=pl.BlockSpec(memory_space=pltpu.VMEM),
        scratch_shapes=[
            pltpu.SemaphoreType.DMA,
            pltpu.SemaphoreType.DMA((shards,)),
            pltpu.SemaphoreType.DMA((shards,)),
            pltpu.SemaphoreType.DMA((bits, shards, 2)),
            pltpu.SemaphoreType.DMA((bits, shards, 2)),
        ],
        compiler_params=pltpu.CompilerParams(
            collective_id=0, has_side_effects=True, vmem_limit_bytes=24 << 20
        ),
        name="gather_weights",
    )(packed)


def reduce_kernel(bits, shards, given, out, total, *rest):
    landing = rest[: 2 * bits]
    z_land, local_sem, z_send, z_recv, rs_send, rs_recv, ag_send, ag_recv = rest[2 * bits :]
    mine, flipped, z, others = partners(bits, shards)
    greet(bits, shards, flipped, others)
    orders = bit_orders(bits)
    copies = {}
    sent = []
    for t in range(bits):
        for half in range(2):
            bit = orders[half][bits - 1 - t]
            free = orders[half][: bits - 1 - t]
            theirs = list(mine)
            theirs[bit] = 1 - mine[bit]
            land = landing[2 * t + half]
            if t > 0:
                before = landing[2 * t - 2 + half]
                copies[t - 1, half].wait_recv()
                keep = (slice(None),) + bit_index(bits, mine, orders[half][: bits - t]) + (half,)
                source = given if t == 1 else total
                total[keep] = (source[keep].astype(F32) + before[...].astype(F32)).astype(BF16)
            where = (slice(None),) + bit_index(bits, theirs, free) + (half,)
            copies[t, half] = remote(
                (given if t == 0 else total).at[where],
                land,
                rs_send.at[t, half],
                rs_recv.at[t, half],
                {"rep": flipped[bit]},
            )
            sent.append(copies[t, half])
    piece = bit_index(bits, mine, ())
    for half in range(2):
        copies[bits - 1, half].wait_recv()
        keep = (slice(None),) + piece + (half,)
        total[keep] = (
            total[keep].astype(F32) + landing[2 * bits - 2 + half][...].astype(F32)
        ).astype(BF16)
    hops = {}
    for d in range(1, shards):
        hops[d] = remote(
            total.at[(others[d],) + piece],
            z_land.at[d],
            z_send.at[d],
            z_recv.at[d],
            {"shard": others[d]},
        )
        sent.append(hops[d])
    value = total[(z,) + piece].astype(F32)
    for d in range(1, shards):
        hops[d].wait_recv()
        value = value + z_land[d].astype(F32)
    out[piece] = value.astype(BF16)
    for t in range(bits):
        for half in range(2):
            if t > 0:
                copies[t - 1, half, "ag"].wait_recv()
            bit = orders[half][t]
            where = bit_index(bits, mine, orders[half][:t]) + (half,)
            copies[t, half, "ag"] = remote(
                out.at[where],
                out.at[where],
                ag_send.at[t, half],
                ag_recv.at[t, half],
                {"rep": flipped[bit]},
            )
            sent.append(copies[t, half, "ag"])
    for half in range(2):
        copies[bits - 1, half, "ag"].wait_recv()
    for copy in sent:
        copy.wait_send()


def reduce_grads(packed, bits, shards):
    tail = packed.shape[-2:]
    landing = []
    for t in range(bits):
        for half in range(2):
            landing.append(pltpu.VMEM((shards,) + (2,) * (bits - 1 - t) + tail, BF16))
    dma = pltpu.SemaphoreType.DMA
    return pl.pallas_call(
        functools.partial(reduce_kernel, bits, shards),
        out_shape=jax.ShapeDtypeStruct(packed.shape[1:], BF16),
        in_specs=[pl.BlockSpec(memory_space=pltpu.VMEM)],
        out_specs=pl.BlockSpec(memory_space=pltpu.VMEM),
        scratch_shapes=[
            pltpu.VMEM(packed.shape, BF16),
            *landing,
            pltpu.VMEM((shards, 2) + tail, BF16),
            dma,
            dma((shards,)),
            dma((shards,)),
            dma((bits, 2)),
            dma((bits, 2)),
            dma((bits, 2)),
            dma((bits, 2)),
        ],
        compiler_params=pltpu.CompilerParams(
            collective_id=1, has_side_effects=True, vmem_limit_bytes=40 << 20
        ),
        name="reduce_grads",
    )(packed)


def norm_forward(values, gain, shift):
    centre = jnp.mean(values, axis=-1, keepdims=True)
    centred = values - centre
    inv_std = lax.rsqrt(jnp.mean(centred * centred, axis=-1, keepdims=True) + 1e-06)
    normed = centred * inv_std
    return normed * gain + shift, normed, inv_std


def norm_backward(grad_out, normed, inv_std, gain):
    scaled = grad_out * gain
    return inv_std * (
        scaled
        - jnp.mean(scaled, axis=-1, keepdims=True)
        - normed * jnp.mean(scaled * normed, axis=-1, keepdims=True)
    )


def gelu_parts(values):
    normal_cdf = 0.5 * (1.0 + lax.erf(values * inverse_root_two))
    slope = normal_cdf + values * jnp.exp(-0.5 * values * values) * inverse_root_tau
    return values * normal_cdf, slope


def dot(a, b):
    return lax.dot_general(a, b, (((1,), (0,)), ((), ())), preferred_element_type=F32)


def dot_nt(a, b):
    return lax.dot_general(a, b, (((1,), (1,)), ((), ())), preferred_element_type=F32)


def dot_tn(a, b):
    return lax.dot_general(a, b, (((0,), (0,)), ((), ())), preferred_element_type=F32)


def column_sum(values):
    return jnp.sum(values, axis=0, keepdims=True)


def layer_kernel(
    shards,
    x_ref,
    cot_ref,
    w_ref,
    out_ref,
    gtok_ref,
    g_ref,
    flat,
    xpad,
    cpad,
    wqkv,
    wo,
    w1,
    w2,
    h1s,
    mixs,
    h2s,
    acts,
    cots,
    gps,
    grs,
    gqs,
    probs,
    vacc,
):
    width = x_ref.shape[1]
    rows = width // shards
    hidden = w2.shape[0]
    slabs = hidden // width
    images = x_ref.shape[0] // SEQ
    padded = xpad.shape[0] // images
    base = (4 + 2 * slabs) * rows
    for z in range(shards):
        own = slice(z * rows, (z + 1) * rows)
        for c in range(3):
            wqkv[own, c * width : (c + 1) * width] = w_ref[z, c * rows : (c + 1) * rows, :]
        wo[own, :] = w_ref[z, 3 * rows : 4 * rows, :]
        for j in range(slabs):
            w1[own, j * width : (j + 1) * width] = w_ref[z, (4 + j) * rows : (5 + j) * rows, :]
        deep = slabs * rows
        w2[z * deep : (z + 1) * deep, :] = w_ref[z, (4 + slabs) * rows : base, :]
    vec = w_ref[0, base : base + VEC_ROWS, :].astype(F32)
    for z in range(1, shards):
        vec = vec + w_ref[z, base : base + VEC_ROWS, :].astype(F32)
    vacc[...] = jnp.zeros_like(vacc)
    for source, target in ((x_ref, xpad), (cot_ref, cpad)):
        target[...] = jnp.zeros_like(target)
        flat[...] = source[...].astype(F32)
        for i in range(images):
            target[i * padded : i * padded + SEQ, :] = flat[i * SEQ : (i + 1) * SEQ, :]

    gain_one, shift_one, q_shift, v_shift = (vec[r : r + 1, :] for r in range(4))
    out_shift, gain_two, shift_two, fc2_shift = (vec[r : r + 1, :] for r in range(4, 8))

    def image(i, carry):
        here = pl.ds(pl.multiple_of(i * padded, 16), padded)
        x_float = xpad[here, :]
        cot_float = cpad[here, :]
        cot_b = cot_float.astype(BF16)
        cots[here, :] = cot_b
        norm_one, normed_one, inv_one = norm_forward(x_float, gain_one, shift_one)
        hidden_one = norm_one.astype(BF16)
        h1s[here, :] = hidden_one
        query = (dot(hidden_one, wqkv[:, :width]) + q_shift).astype(BF16)
        keys = dot(hidden_one, wqkv[:, width : 2 * width]).astype(BF16)
        vals = (dot(hidden_one, wqkv[:, 2 * width :]) + v_shift).astype(BF16)
        outside = lax.broadcasted_iota(jnp.int32, (padded, padded), 1) >= SEQ
        pieces = []
        for h in range(HEADS):
            cols = slice(h * HEAD_DIM, (h + 1) * HEAD_DIM)
            scores = dot_nt(query[:, cols], keys[:, cols]) * float(HEAD_DIM) ** (-0.5)
            scores = jnp.where(outside, -1e30, scores)
            top = jnp.max(scores, axis=-1, keepdims=True)
            grown = jnp.exp(scores - top)
            prob = grown * (1.0 / jnp.sum(grown, axis=-1, keepdims=True))
            probs[h] = prob
            pieces.append(dot(prob.astype(BF16), vals[:, cols]).astype(BF16))
        mixed = jnp.concatenate(pieces, axis=1)
        mixs[here, :] = mixed
        resid = x_float + dot(mixed, wo[...]) + out_shift
        norm_two, normed_two, inv_two = norm_forward(resid, gain_two, shift_two)
        hidden_two = norm_two.astype(BF16)
        h2s[here, :] = hidden_two
        total = resid + fc2_shift
        grad_h2 = jnp.zeros_like(resid)
        for j in range(slabs):
            cols = slice(j * width, (j + 1) * width)
            pre = dot(hidden_two, w1[:, cols]) + vec[8 + j : 9 + j, :]
            act, slope = gelu_parts(pre)
            act_b = act.astype(BF16)
            acts[here, cols] = act_b
            total = total + dot(act_b, w2[cols, :])
            grad_pre = dot_nt(cot_b, w2[cols, :]) * slope
            grad_pre_b = grad_pre.astype(BF16)
            gps[here, cols] = grad_pre_b
            vacc[8 + j : 9 + j, :] += column_sum(grad_pre)
            grad_h2 = grad_h2 + dot_nt(grad_pre_b, w1[:, cols])
        grad_resid = cot_float + norm_backward(grad_h2, normed_two, inv_two, gain_two)
        vacc[5:6, :] += column_sum(grad_h2 * normed_two)
        vacc[6:7, :] += column_sum(grad_h2)
        vacc[7:8, :] += column_sum(cot_float)
        vacc[4:5, :] += column_sum(grad_resid)
        cpad[here, :] = total
        grad_resid_b = grad_resid.astype(BF16)
        grs[here, :] = grad_resid_b
        grad_mixed = dot_nt(grad_resid_b, wo[...]).astype(BF16)
        dq, dk, dv = [], [], []
        for h in range(HEADS):
            cols = slice(h * HEAD_DIM, (h + 1) * HEAD_DIM)
            prob = probs[h]
            grad_head = grad_mixed[:, cols]
            dv.append(dot_tn(prob.astype(BF16), grad_head))
            grad_prob = dot_nt(grad_head, vals[:, cols])
            inner = jnp.sum(prob * grad_prob, axis=-1, keepdims=True)
            grad_scores = (prob * (grad_prob - inner) * float(HEAD_DIM) ** (-0.5)).astype(BF16)
            dq.append(dot(grad_scores, keys[:, cols]))
            dk.append(dot_tn(grad_scores, query[:, cols]))
        grad_h1 = jnp.zeros_like(resid)
        for c, parts in enumerate((dq, dk, dv)):
            grad = jnp.concatenate(parts, axis=1)
            if c == 0:
                vacc[2:3, :] += column_sum(grad)
            if c == 2:
                vacc[3:4, :] += column_sum(grad)
            grad_b = grad.astype(BF16)
            cols = slice(c * width, (c + 1) * width)
            gqs[here, cols] = grad_b
            grad_h1 = grad_h1 + dot_nt(grad_b, wqkv[:, cols])
        vacc[0:1, :] += column_sum(grad_h1 * normed_one)
        vacc[1:2, :] += column_sum(grad_h1)
        xpad[here, :] = grad_resid + norm_backward(grad_h1, normed_one, inv_one, gain_one)
        return carry

    lax.fori_loop(0, images, image, 0)

    for source, target in ((xpad, gtok_ref), (cpad, out_ref)):
        for i in range(images):
            flat[i * SEQ : (i + 1) * SEQ, :] = source[i * padded : i * padded + SEQ, :]
        target[...] = flat[...].astype(BF16)

    def put(grad, slab):
        for z in range(shards):
            g_ref[z, slab * rows : (slab + 1) * rows, :] = grad[z * rows : (z + 1) * rows].astype(BF16)

    for c in range(3):
        put(dot_tn(h1s[...], gqs[:, c * width : (c + 1) * width]), c)
    put(dot_tn(mixs[...], grs[...]), 3)
    for j in range(slabs):
        put(dot_tn(h2s[...], gps[:, j * width : (j + 1) * width]), 4 + j)
    for z in range(shards):
        deep = slabs * rows
        grad = dot_tn(acts[:, z * deep : (z + 1) * deep], cots[...])
        g_ref[z, (4 + slabs) * rows : base, :] = grad.astype(BF16)
        g_ref[z, base:, :] = jnp.zeros_like(g_ref[z, base:, :])
        g_ref[z, base : base + VEC_ROWS, :] = vacc[...].astype(BF16)


def layer(tokens, cotangent, weights, hidden):
    count, width = tokens.shape
    shards, total, _ = weights.shape
    images = count // SEQ
    long = images * (-(-SEQ // 16) * 16)
    vmem = pl.BlockSpec(memory_space=pltpu.VMEM)
    return pl.pallas_call(
        functools.partial(layer_kernel, shards),
        out_shape=(
            jax.ShapeDtypeStruct(tokens.shape, BF16),
            jax.ShapeDtypeStruct(tokens.shape, BF16),
            jax.ShapeDtypeStruct(weights.shape, BF16),
        ),
        in_specs=[vmem] * 3,
        out_specs=(vmem,) * 3,
        scratch_shapes=[
            pltpu.VMEM((count, width), F32),
            pltpu.VMEM((long, width), F32),
            pltpu.VMEM((long, width), F32),
            pltpu.VMEM((width, 3 * width), BF16),
            pltpu.VMEM((width, width), BF16),
            pltpu.VMEM((width, hidden), BF16),
            pltpu.VMEM((hidden, width), BF16),
            pltpu.VMEM((long, width), BF16),
            pltpu.VMEM((long, width), BF16),
            pltpu.VMEM((long, width), BF16),
            pltpu.VMEM((long, hidden), BF16),
            pltpu.VMEM((long, width), BF16),
            pltpu.VMEM((long, hidden), BF16),
            pltpu.VMEM((long, width), BF16),
            pltpu.VMEM((long, 3 * width), BF16),
            pltpu.VMEM((HEADS, long // images, long // images), F32),
            pltpu.VMEM((VEC_ROWS, width), F32),
        ],
        compiler_params=pltpu.CompilerParams(vmem_limit_bytes=60 << 20),
        name="layer",
    )(tokens, cotangent, weights)


def per_device(
    tokens,
    cotangent,
    ln1_gain,
    ln1_bias,
    w_qkv,
    bias_qv,
    w_out,
    bias_out,
    ln2_gain,
    ln2_bias,
    w_fc1,
    bias_fc1,
    w_fc2,
    bias_fc2,
):
    replicas, shards = lax.axis_size("rep"), lax.axis_size("shard")
    bits = replicas.bit_length() - 1
    factor = float(tokens.shape[0] * replicas * shards) ** (-0.5)
    rows, width = w_out.shape
    hidden = w_fc1.shape[1]
    slabs = hidden // width
    base = (4 + 2 * slabs) * rows
    unit = 32 * replicas
    total = -(-(base + VEC_ROWS) // unit) * unit
    z = lax.axis_index("shard")
    small = jnp.stack(
        [ln1_gain, ln1_bias, bias_qv[0], bias_qv[1], bias_out, ln2_gain, ln2_bias, bias_fc2]
    )
    vec = jnp.zeros((total - base, width), BF16)
    vec = lax.dynamic_update_slice(vec, small, (0, z * rows))
    vec = lax.dynamic_update_slice(vec, bias_fc1[None, :], (8 + z, 0))
    parts = [w_qkv[:, c * width : (c + 1) * width] for c in range(3)] + [w_out]
    parts += [w_fc1[:, j * width : (j + 1) * width] for j in range(slabs)] + [w_fc2, vec]
    packed = jnp.concatenate(parts, axis=0)
    pieces = (2,) * (bits + 1) + (total // (2 * replicas), width)
    weights = gather(packed.reshape(pieces), bits, shards).reshape(shards, total, width)
    layer_out, grad_tok, grads = layer(tokens, cotangent, weights, hidden)
    owned = reduce_grads(grads.reshape((shards,) + pieces), bits, shards).reshape(total, width)

    def slab(j):
        return owned[j * rows : (j + 1) * rows, :]

    def scale(value):
        return value.astype(F32) * factor

    def vector(r):
        return lax.dynamic_slice(owned, (base + r, z * rows), (1, rows))

    fc1_shift = lax.dynamic_slice(owned, (base + 8 + z, 0), (1, width))[0]
    return (
        layer_out,
        grad_tok,
        scale(vector(0)[0]),
        scale(vector(1)[0]),
        scale(jnp.concatenate([slab(c) for c in range(3)], axis=1)),
        scale(jnp.concatenate([vector(2), vector(3)], axis=0)),
        scale(slab(3)),
        scale(vector(4)[0]),
        scale(vector(5)[0]),
        scale(vector(6)[0]),
        scale(jnp.concatenate([slab(4 + j) for j in range(slabs)], axis=1)),
        scale(fc1_shift),
        scale(owned[(4 + slabs) * rows : base, :]),
        scale(vector(7)[0]),
    )


def solution(mesh):
    both = P(("rep", "shard"), None)
    lone = P("shard")
    flat = P("shard", None)
    pair = P(None, "shard")
    params = (lone, lone, flat, pair, flat, lone, lone, lone, flat, lone, flat, lone)
    return jax.shard_map(
        per_device,
        mesh=mesh,
        in_specs=(both, both) + params,
        out_specs=(both, both) + params,
        check_vma=False,
    )
```

```python
import functools

import jax
import jax.numpy as jnp
from jax import lax
from jax.experimental import pallas as pl
from jax.experimental.pallas import tpu as pltpu
from jax.sharding import PartitionSpec as P

HEADS = 6
HEAD_DIM = 64
SEQ = 197
VEC_ROWS = 16

F32 = jnp.float32
BF16 = jnp.bfloat16
inverse_root_two = 0.7071067811865476
inverse_root_tau = 0.3989422804014327


def bit_orders(bits):
    high = list(range(1, bits))
    return (high + [0], high[::-1] + [0])


def partners(bits, shards):
    me = lax.axis_index("rep")
    mine = [lax.rem(lax.div(me, 2**b), 2) for b in range(bits)]
    flipped = [me + (1 - 2 * mine[b]) * 2**b for b in range(bits)]
    z = lax.axis_index("shard")
    others = [lax.rem(z + d, shards) for d in range(shards)]
    return mine, flipped, z, others


def greet(bits, shards, flipped, others):
    barrier = pltpu.get_barrier_semaphore()
    for b in range(bits):
        pl.semaphore_signal(
            barrier, inc=1, device_id={"rep": flipped[b]}, device_id_type=pl.DeviceIdType.MESH
        )
    for d in range(1, shards):
        pl.semaphore_signal(
            barrier, inc=1, device_id={"shard": others[d]}, device_id_type=pl.DeviceIdType.MESH
        )
    pl.semaphore_wait(barrier, bits + shards - 1)


def remote(src, dst, send, recv, where):
    copy = pltpu.make_async_remote_copy(
        src_ref=src,
        dst_ref=dst,
        send_sem=send,
        recv_sem=recv,
        device_id=where,
        device_id_type=pl.DeviceIdType.MESH,
    )
    copy.start()
    return copy


def bit_index(bits, mine, free):
    return tuple(slice(None) if b in free else mine[b] for b in reversed(range(bits)))


def norm_forward(values, gain, shift):
    centre = jnp.mean(values, axis=-1, keepdims=True)
    centred = values - centre
    inv_std = lax.rsqrt(jnp.mean(centred * centred, axis=-1, keepdims=True) + 1e-06)
    normed = centred * inv_std
    return normed * gain + shift, normed, inv_std


def norm_backward(grad_out, normed, inv_std, gain):
    scaled = grad_out * gain
    return inv_std * (
        scaled
        - jnp.mean(scaled, axis=-1, keepdims=True)
        - normed * jnp.mean(scaled * normed, axis=-1, keepdims=True)
    )


def gelu_parts(values):
    normal_cdf = 0.5 * (1.0 + lax.erf(values * inverse_root_two))
    slope = normal_cdf + values * jnp.exp(-0.5 * values * values) * inverse_root_tau
    return values * normal_cdf, slope


def dot(a, b):
    return lax.dot_general(a, b, (((1,), (0,)), ((), ())), preferred_element_type=F32)


def dot_nt(a, b):
    return lax.dot_general(a, b, (((1,), (1,)), ((), ())), preferred_element_type=F32)


def dot_tn(a, b):
    return lax.dot_general(a, b, (((0,), (0,)), ((), ())), preferred_element_type=F32)


def column_sum(values):
    return jnp.sum(values, axis=0, keepdims=True)


def chunks(bits, unit, start, count):
    found = []
    row = start
    while row < start + count:
        number, inside = divmod(row, unit)
        length = min(unit - inside, start + count - row)
        index = tuple((number >> b) & 1 for b in reversed(range(bits + 1)))
        found.append((index, slice(inside, inside + length), row - start, length))
        row += length
    return found


class Gather:
    def __init__(self, bits, shards, place, own, full, sems):
        self.bits, self.shards, self.own, self.full = bits, shards, own, full
        self.mine, self.flipped, self.z, self.others = place
        self.local_sem, self.z_send, self.z_recv, self.send, self.recv = sems
        self.orders = bit_orders(bits)
        self.hops, self.copies = {}, {}

    def start(self):
        piece = bit_index(self.bits, self.mine, ())
        for d in range(1, self.shards):
            self.hops[d] = remote(
                self.own.at[piece],
                self.full.at[(self.z,) + piece],
                self.z_send.at[d],
                self.z_recv.at[d],
                {"shard": self.others[d]},
            )
        self.local = pltpu.make_async_copy(self.own, self.full.at[self.z], self.local_sem)
        self.local.start()

    def step(self, t):
        for d in range(1, self.shards):
            source = lax.rem(self.z - d + self.shards, self.shards)
            for half in range(2):
                if t > 0:
                    self.copies[t - 1, d, half].wait_recv()
                elif half == 0:
                    self.hops[d].wait_recv()
                order = self.orders[half]
                where = (source,) + bit_index(self.bits, self.mine, order[:t]) + (half,)
                self.copies[t, d, half] = remote(
                    self.full.at[where],
                    self.full.at[where],
                    self.send.at[t, d, half],
                    self.recv.at[t, d, half],
                    {"rep": self.flipped[order[t]]},
                )

    def finish(self):
        for d in range(1, self.shards):
            for half in range(2):
                self.copies[self.bits - 1, d, half].wait_recv()
        self.local.wait()

    def drain(self):
        for copy in list(self.hops.values()) + list(self.copies.values()):
            copy.wait_send()


class Reduce:
    def __init__(self, bits, shards, place, total, out, landing, z_land, sems):
        self.bits, self.shards, self.total, self.out = bits, shards, total, out
        self.mine, self.flipped, self.z, self.others = place
        self.landing, self.z_land = landing, z_land
        self.z_send, self.z_recv, self.rs_send, self.rs_recv, self.ag_send, self.ag_recv = sems
        self.orders = bit_orders(bits)
        self.copies, self.gathers, self.hops = {}, {}, {}

    def add(self, t, half):
        self.copies[t, half].wait_recv()
        free = self.orders[half][: self.bits - 1 - t]
        keep = (slice(None),) + bit_index(self.bits, self.mine, free) + (half,)
        land = self.landing[2 * t + half]
        self.total[keep] = (self.total[keep].astype(F32) + land[...].astype(F32)).astype(BF16)

    def step(self, t):
        for half in range(2):
            if t > 0:
                self.add(t - 1, half)
            bit = self.orders[half][self.bits - 1 - t]
            theirs = list(self.mine)
            theirs[bit] = 1 - self.mine[bit]
            free = self.orders[half][: self.bits - 1 - t]
            where = (slice(None),) + bit_index(self.bits, theirs, free) + (half,)
            self.copies[t, half] = remote(
                self.total.at[where],
                self.landing[2 * t + half],
                self.rs_send.at[t, half],
                self.rs_recv.at[t, half],
                {"rep": self.flipped[bit]},
            )

    def hop(self):
        for half in range(2):
            self.add(self.bits - 1, half)
        piece = bit_index(self.bits, self.mine, ())
        for d in range(1, self.shards):
            self.hops[d] = remote(
                self.total.at[(self.others[d],) + piece],
                self.z_land.at[d],
                self.z_send.at[d],
                self.z_recv.at[d],
                {"shard": self.others[d]},
            )

    def own(self):
        piece = bit_index(self.bits, self.mine, ())
        value = self.total[(self.z,) + piece].astype(F32)
        for d in range(1, self.shards):
            self.hops[d].wait_recv()
            value = value + self.z_land[d].astype(F32)
        self.out[piece] = value.astype(BF16)

    def spread(self, t):
        for half in range(2):
            if t > 0:
                self.gathers[t - 1, half].wait_recv()
            order = self.orders[half]
            where = bit_index(self.bits, self.mine, order[:t]) + (half,)
            self.gathers[t, half] = remote(
                self.out.at[where],
                self.out.at[where],
                self.ag_send.at[t, half],
                self.ag_recv.at[t, half],
                {"rep": self.flipped[order[t]]},
            )

    def finish(self):
        for half in range(2):
            self.gathers[self.bits - 1, half].wait_recv()
        for group in (self.copies, self.hops, self.gathers):
            for copy in group.values():
                copy.wait_send()


def group_rows(needed, replicas):
    unit = 32 * replicas
    return -(-needed // unit) * unit


def layer_kernel(bits, shards, *refs):
    x_ref, cot_ref, vec_ref, wqkv_ref, wo_ref, w1_ref, w2_ref = refs[:7]
    out_ref, gtok_ref, owned_a, owned_f = refs[7:11]
    (flat, xpad, cpad, wqkv, wo, w1, w2, h1s, mixs, h2s, acts, cots, gps, grs, gqs) = refs[11:26]
    (qs, ks, vs, resids, greds, probs, vacc, own_a, own_f, full_a, full_f) = refs[26:37]
    z_land_a, z_land_f, pack_sem = refs[37:40]
    rest = refs[40:]
    g_a, g_f = full_a, full_f
    landing_a, landing_f, sems = rest[: 2 * bits], rest[2 * bits : 4 * bits], rest[4 * bits :]

    width = x_ref.shape[1]
    rows = width // shards
    hidden = w2.shape[0]
    slabs = hidden // width
    deep = slabs * rows
    images = x_ref.shape[0] // SEQ
    padded = xpad.shape[0] // images
    unit_a, unit_f = own_a.shape[-2], own_f.shape[-2]

    place = partners(bits, shards)
    greet(bits, shards, place[1], place[3])

    def pack(own, unit, sources, first):
        started = []
        for source, column, start, count in sources:
            for index, inside, offset, length in chunks(bits, unit, start, count):
                copy = pltpu.make_async_copy(
                    source.at[offset : offset + length, column : column + width],
                    own.at[index + (inside,)],
                    pack_sem.at[first + len(started)],
                )
                copy.start()
                started.append(copy)
        return started

    sources_a = [(wqkv_ref, c * width, c * rows, rows) for c in range(3)]
    sources_a += [(wo_ref, 0, 3 * rows, rows), (vec_ref, 0, 4 * rows, VEC_ROWS)]
    sources_f = [(w1_ref, j * width, j * rows, rows) for j in range(slabs)]
    sources_f += [(w2_ref, 0, deep, deep)]
    packs_a = pack(own_a, unit_a, sources_a, 0)
    packs_f = pack(own_f, unit_f, sources_f, len(packs_a))
    gather_a = Gather(bits, shards, place, own_a, full_a, sems[:5])
    gather_f = Gather(bits, shards, place, own_f, full_f, sems[5:10])
    for copy in packs_a:
        copy.wait()
    gather_a.start()
    for copy in packs_f:
        copy.wait()

    vacc[...] = jnp.zeros_like(vacc)
    for source, target in ((x_ref, xpad), (cot_ref, cpad)):
        target[...] = jnp.zeros_like(target)
        flat[...] = source[...].astype(F32)
        for i in range(images):
            target[i * padded : i * padded + SEQ, :] = flat[i * SEQ : (i + 1) * SEQ, :]
    gather_a.step(0)
    gather_f.start()
    for t in range(1, bits):
        gather_a.step(t)
    gather_a.finish()

    def unpack(full, unit, pairs):
        for target, row, column, start, count in pairs:
            for z in range(shards):
                for index, inside, offset, length in chunks(bits, unit, start, count):
                    at = row(z) + offset
                    target[at : at + length, column : column + width] = full[(z,) + index + (inside,)]

    thin = lambda z: z * rows
    thick = lambda z: z * deep
    unpack(full_a, unit_a, [(wqkv, thin, c * width, c * rows, rows) for c in range(3)])
    unpack(full_a, unit_a, [(wo, thin, 0, 3 * rows, rows)])

    def vec_of(z):
        index, inside, _, _ = chunks(bits, unit_a, 4 * rows, VEC_ROWS)[0]
        return full_a[(z,) + index + (inside,)].astype(F32)

    vec = vec_of(0)
    for z in range(1, shards):
        vec = vec + vec_of(z)
    gain_one, shift_one, q_shift, v_shift = (vec[r : r + 1, :] for r in range(4))
    out_shift, gain_two, shift_two, fc2_shift = (vec[r : r + 1, :] for r in range(4, 8))

    def rows_of(i):
        return pl.ds(pl.multiple_of(i * padded, 16), padded)

    def attend(i, carry):
        here = rows_of(i)
        x_float = xpad[here, :]
        norm_one, _, _ = norm_forward(x_float, gain_one, shift_one)
        hidden_one = norm_one.astype(BF16)
        h1s[here, :] = hidden_one
        query = (dot(hidden_one, wqkv[:, :width]) + q_shift).astype(BF16)
        keys = dot(hidden_one, wqkv[:, width : 2 * width]).astype(BF16)
        vals = (dot(hidden_one, wqkv[:, 2 * width :]) + v_shift).astype(BF16)
        qs[here, :] = query
        ks[here, :] = keys
        vs[here, :] = vals
        outside = lax.broadcasted_iota(jnp.int32, (padded, padded), 1) >= SEQ
        pieces = []
        for h in range(HEADS):
            cols = slice(h * HEAD_DIM, (h + 1) * HEAD_DIM)
            scores = dot_nt(query[:, cols], keys[:, cols]) * float(HEAD_DIM) ** (-0.5)
            scores = jnp.where(outside, -1e30, scores)
            top = jnp.max(scores, axis=-1, keepdims=True)
            grown = jnp.exp(scores - top)
            prob = grown * (1.0 / jnp.sum(grown, axis=-1, keepdims=True))
            probs[i, h] = prob
            pieces.append(dot(prob.astype(BF16), vals[:, cols]).astype(BF16))
        mixed = jnp.concatenate(pieces, axis=1)
        mixs[here, :] = mixed
        resids[here, :] = x_float + dot(mixed, wo[...]) + out_shift
        return carry

    gather_f.step(0)
    halfway = images // 2
    lax.fori_loop(0, halfway, attend, 0)
    for t in range(1, bits - 1):
        gather_f.step(t)
    lax.fori_loop(halfway, images, attend, 0)
    gather_f.step(bits - 1)
    gather_f.finish()
    unpack(full_f, unit_f, [(w1, thin, j * width, j * rows, rows) for j in range(slabs)])
    for z in range(shards):
        for index, inside, offset, length in chunks(bits, unit_f, deep, deep):
            at = z * deep + offset
            w2[at : at + length, :] = full_f[(z,) + index + (inside,)]

    def feed(i, carry):
        here = rows_of(i)
        resid = resids[here, :]
        cot_float = cpad[here, :]
        cot_b = cot_float.astype(BF16)
        cots[here, :] = cot_b
        norm_two, normed_two, inv_two = norm_forward(resid, gain_two, shift_two)
        hidden_two = norm_two.astype(BF16)
        h2s[here, :] = hidden_two
        total = resid + fc2_shift
        grad_h2 = jnp.zeros_like(resid)
        for j in range(slabs):
            cols = slice(j * width, (j + 1) * width)
            pre = dot(hidden_two, w1[:, cols]) + vec[8 + j : 9 + j, :]
            act, slope = gelu_parts(pre)
            act_b = act.astype(BF16)
            acts[here, cols] = act_b
            total = total + dot(act_b, w2[cols, :])
            grad_pre = dot_nt(cot_b, w2[cols, :]) * slope
            grad_pre_b = grad_pre.astype(BF16)
            gps[here, cols] = grad_pre_b
            vacc[8 + j : 9 + j, :] += column_sum(grad_pre)
            grad_h2 = grad_h2 + dot_nt(grad_pre_b, w1[:, cols])
        grad_resid = cot_float + norm_backward(grad_h2, normed_two, inv_two, gain_two)
        vacc[5:6, :] += column_sum(grad_h2 * normed_two)
        vacc[6:7, :] += column_sum(grad_h2)
        vacc[7:8, :] += column_sum(cot_float)
        vacc[4:5, :] += column_sum(grad_resid)
        cpad[here, :] = total
        greds[here, :] = grad_resid
        grs[here, :] = grad_resid.astype(BF16)
        return carry

    lax.fori_loop(0, images, feed, 0)

    def put(packed, unit, grad, per, start, count):
        for z in range(shards):
            for index, inside, offset, length in chunks(bits, unit, start, count):
                at = z * per + offset
                packed[(z,) + index + (inside,)] = grad[at : at + length].astype(BF16)

    gather_f.drain()
    for j in range(slabs):
        put(g_f, unit_f, dot_tn(h2s[...], gps[:, j * width : (j + 1) * width]), rows, j * rows, rows)
    for z in range(shards):
        grad = dot_tn(acts[:, z * deep : (z + 1) * deep], cots[...])
        for index, inside, offset, length in chunks(bits, unit_f, deep, deep):
            g_f[(z,) + index + (inside,)] = grad[offset : offset + length].astype(BF16)

    def blank(packed, unit, start):
        count = unit * 2 ** (bits + 1) - start
        for index, inside, _, length in chunks(bits, unit, start, count):
            for z in range(shards):
                packed[(z,) + index + (inside,)] = jnp.zeros((length, width), BF16)

    blank(g_f, unit_f, 2 * deep)
    reduce_f = Reduce(bits, shards, place, g_f, owned_f, landing_f, z_land_f, sems[10:16])
    reduce_a = Reduce(bits, shards, place, g_a, owned_a, landing_a, z_land_a, sems[16:22])
    reduce_f.step(0)

    def attend_back(i, carry):
        here = rows_of(i)
        grad_resid = greds[here, :]
        query, keys, vals = qs[here, :], ks[here, :], vs[here, :]
        grad_mixed = dot_nt(grs[here, :], wo[...]).astype(BF16)
        dq, dk, dv = [], [], []
        for h in range(HEADS):
            cols = slice(h * HEAD_DIM, (h + 1) * HEAD_DIM)
            prob = probs[i, h]
            grad_head = grad_mixed[:, cols]
            dv.append(dot_tn(prob.astype(BF16), grad_head))
            grad_prob = dot_nt(grad_head, vals[:, cols])
            inner = jnp.sum(prob * grad_prob, axis=-1, keepdims=True)
            grad_scores = (prob * (grad_prob - inner) * float(HEAD_DIM) ** (-0.5)).astype(BF16)
            dq.append(dot(grad_scores, keys[:, cols]))
            dk.append(dot_tn(grad_scores, query[:, cols]))
        grad_h1 = jnp.zeros_like(grad_resid)
        for c, parts in enumerate((dq, dk, dv)):
            grad = jnp.concatenate(parts, axis=1)
            if c == 0:
                vacc[2:3, :] += column_sum(grad)
            if c == 2:
                vacc[3:4, :] += column_sum(grad)
            grad_b = grad.astype(BF16)
            cols = slice(c * width, (c + 1) * width)
            gqs[here, cols] = grad_b
            grad_h1 = grad_h1 + dot_nt(grad_b, wqkv[:, cols])
        _, normed_one, inv_one = norm_forward(xpad[here, :], gain_one, shift_one)
        vacc[0:1, :] += column_sum(grad_h1 * normed_one)
        vacc[1:2, :] += column_sum(grad_h1)
        xpad[here, :] = grad_resid + norm_backward(grad_h1, normed_one, inv_one, gain_one)
        return carry

    lax.fori_loop(0, halfway, attend_back, 0)
    reduce_f.step(1)
    lax.fori_loop(halfway, images, attend_back, 0)
    for t in range(2, bits):
        reduce_f.step(t)
    gather_a.drain()
    for c in range(3):
        put(g_a, unit_a, dot_tn(h1s[...], gqs[:, c * width : (c + 1) * width]), rows, c * rows, rows)
    put(g_a, unit_a, dot_tn(mixs[...], grs[...]), rows, 3 * rows, rows)
    blank(g_a, unit_a, 4 * rows + VEC_ROWS)
    index, inside, _, _ = chunks(bits, unit_a, 4 * rows, VEC_ROWS)[0]
    for z in range(shards):
        g_a[(z,) + index + (inside,)] = vacc[...].astype(BF16)
    reduce_a.step(0)
    reduce_f.hop()
    for t in range(1, bits):
        reduce_a.step(t)
    for source, target in ((xpad, gtok_ref), (cpad, out_ref)):
        for i in range(images):
            flat[i * SEQ : (i + 1) * SEQ, :] = source[i * padded : i * padded + SEQ, :]
        target[...] = flat[...].astype(BF16)
    reduce_f.own()
    reduce_f.spread(0)
    reduce_a.hop()
    for t in range(1, bits):
        reduce_f.spread(t)
    reduce_a.own()
    for t in range(bits):
        reduce_a.spread(t)
    reduce_f.finish()
    reduce_a.finish()


def layer(tokens, cotangent, vec, w_qkv, w_out, w_fc1, w_fc2, bits, shards):
    count, width = tokens.shape
    replicas = 2**bits
    rows = w_out.shape[0]
    hidden = w_fc1.shape[1]
    images = count // SEQ
    padded = -(-SEQ // 16) * 16
    long = images * padded
    rows_a = group_rows(4 * rows + VEC_ROWS, replicas)
    rows_f = group_rows(2 * rows * (hidden // width), replicas)
    twos = (2,) * bits
    tail_a = (rows_a // (2 * replicas), width)
    tail_f = (rows_f // (2 * replicas), width)
    full_a = (shards,) + twos + (2,) + tail_a
    full_f = (shards,) + twos + (2,) + tail_f

    def landing(tail):
        return [
            pltpu.VMEM((shards,) + (2,) * (bits - 1 - t) + tail, BF16)
            for t in range(bits)
            for _ in range(2)
        ]

    dma = pltpu.SemaphoreType.DMA
    gather_sems = [dma, dma((shards,)), dma((shards,)), dma((bits, shards, 2)), dma((bits, shards, 2))]
    reduce_sems = [dma((shards,)), dma((shards,))] + [dma((bits, 2))] * 4
    pieces = 0
    for unit, spans in (
        (tail_a[0], [(c * rows, rows) for c in range(4)] + [(4 * rows, VEC_ROWS)]),
        (tail_f[0], [(j * rows, rows) for j in range(hidden // width)] + [(rows_f0(rows, hidden, width),) * 2]),
    ):
        for start, length in spans:
            pieces += len(chunks(bits, unit, start, length))
    vmem = pl.BlockSpec(memory_space=pltpu.VMEM)
    left = pl.BlockSpec(memory_space=pl.ANY)
    return pl.pallas_call(
        functools.partial(layer_kernel, bits, shards),
        out_shape=(
            jax.ShapeDtypeStruct(tokens.shape, BF16),
            jax.ShapeDtypeStruct(tokens.shape, BF16),
            jax.ShapeDtypeStruct(full_a[1:], BF16),
            jax.ShapeDtypeStruct(full_f[1:], BF16),
        ),
        in_specs=[vmem] * 2 + [left] * 5,
        out_specs=(vmem,) * 4,
        scratch_shapes=[
            pltpu.VMEM((count, width), F32),
            pltpu.VMEM((long, width), F32),
            pltpu.VMEM((long, width), F32),
            pltpu.VMEM((width, 3 * width), BF16),
            pltpu.VMEM((width, width), BF16),
            pltpu.VMEM((width, hidden), BF16),
            pltpu.VMEM((hidden, width), BF16),
            pltpu.VMEM((long, width), BF16),
            pltpu.VMEM((long, width), BF16),
            pltpu.VMEM((long, width), BF16),
            pltpu.VMEM((long, hidden), BF16),
            pltpu.VMEM((long, width), BF16),
            pltpu.VMEM((long, hidden), BF16),
            pltpu.VMEM((long, width), BF16),
            pltpu.VMEM((long, 3 * width), BF16),
            pltpu.VMEM((long, width), BF16),
            pltpu.VMEM((long, width), BF16),
            pltpu.VMEM((long, width), BF16),
            pltpu.VMEM((long, width), F32),
            pltpu.VMEM((long, width), F32),
            pltpu.VMEM((images, HEADS, padded, padded), F32),
            pltpu.VMEM((VEC_ROWS, width), F32),
            pltpu.VMEM(full_a[1:], BF16),
            pltpu.VMEM(full_f[1:], BF16),
            pltpu.VMEM(full_a, BF16),
            pltpu.VMEM(full_f, BF16),
            pltpu.VMEM((shards, 2) + tail_a, BF16),
            pltpu.VMEM((shards, 2) + tail_f, BF16),
            dma((pieces,)),
            *landing(tail_a),
            *landing(tail_f),
            *gather_sems,
            *gather_sems,
            *reduce_sems,
            *reduce_sems,
        ],
        compiler_params=pltpu.CompilerParams(
            collective_id=0, has_side_effects=True, vmem_limit_bytes=62 << 20
        ),
        name="layer",
    )(tokens, cotangent, vec, w_qkv, w_out, w_fc1, w_fc2)


def rows_f0(rows, hidden, width):
    return rows * (hidden // width)


def per_device(
    tokens,
    cotangent,
    ln1_gain,
    ln1_bias,
    w_qkv,
    bias_qv,
    w_out,
    bias_out,
    ln2_gain,
    ln2_bias,
    w_fc1,
    bias_fc1,
    w_fc2,
    bias_fc2,
):
    replicas, shards = lax.axis_size("rep"), lax.axis_size("shard")
    bits = replicas.bit_length() - 1
    factor = float(tokens.shape[0] * replicas * shards) ** (-0.5)
    rows, width = w_out.shape
    slabs = w_fc1.shape[1] // width
    z = lax.axis_index("shard")
    small = jnp.stack(
        [ln1_gain, ln1_bias, bias_qv[0], bias_qv[1], bias_out, ln2_gain, ln2_bias, bias_fc2]
    )
    spread = jnp.concatenate([jnp.tile(small, (1, shards)), jnp.tile(bias_fc1[None, :], (8, 1))])
    row = lax.broadcasted_iota(jnp.int32, spread.shape, 0)
    lane = lax.broadcasted_iota(jnp.int32, spread.shape, 1)
    kept = ((row < 8) & (lane // rows == z)) | (row == 8 + z)
    vec = jnp.where(kept, spread, jnp.zeros_like(spread))
    layer_out, grad_tok, owned_a, owned_f = layer(
        tokens, cotangent, vec, w_qkv, w_out, w_fc1, w_fc2, bits, shards
    )
    owned_a = owned_a.reshape(-1, width)
    owned_f = owned_f.reshape(-1, width)

    def slab(owned, j):
        return owned[j * rows : (j + 1) * rows, :]

    def scale(value):
        return value.astype(F32) * factor

    def vector(r):
        return lax.dynamic_slice(owned_a, (4 * rows + r, z * rows), (1, rows))

    fc1_shift = lax.dynamic_slice(owned_a, (4 * rows + 8 + z, 0), (1, width))[0]
    return (
        layer_out,
        grad_tok,
        scale(vector(0)[0]),
        scale(vector(1)[0]),
        scale(jnp.concatenate([slab(owned_a, c) for c in range(3)], axis=1)),
        scale(jnp.concatenate([vector(2), vector(3)], axis=0)),
        scale(slab(owned_a, 3)),
        scale(vector(4)[0]),
        scale(vector(5)[0]),
        scale(vector(6)[0]),
        scale(jnp.concatenate([slab(owned_f, j) for j in range(slabs)], axis=1)),
        scale(fc1_shift),
        scale(owned_f[slabs * rows : 2 * slabs * rows, :]),
        scale(vector(7)[0]),
    )


def solution(mesh):
    both = P(("rep", "shard"), None)
    lone = P("shard")
    flat = P("shard", None)
    pair = P(None, "shard")
    params = (lone, lone, flat, pair, flat, lone, lone, lone, flat, lone, flat, lone)
    return jax.shard_map(
        per_device,
        mesh=mesh,
        in_specs=(both, both) + params,
        out_specs=(both, both) + params,
        check_vma=False,
    )
```

```python
import functools

import jax
import jax.numpy as jnp
from jax import lax
from jax.experimental import pallas as pl
from jax.experimental.pallas import tpu as pltpu
from jax.sharding import PartitionSpec as P

HEADS = 6
HEAD_DIM = 64
SEQ = 197
VEC_ROWS = 16

F32 = jnp.float32
BF16 = jnp.bfloat16
inverse_root_two = 0.7071067811865476
inverse_root_tau = 0.3989422804014327


def bit_orders(bits):
    high = list(range(1, bits))
    return (high + [0], high[::-1] + [0])


def partners(bits, shards):
    me = lax.axis_index("rep")
    mine = [lax.rem(lax.div(me, 2**b), 2) for b in range(bits)]
    flipped = [me + (1 - 2 * mine[b]) * 2**b for b in range(bits)]
    z = lax.axis_index("shard")
    others = [lax.rem(z + d, shards) for d in range(shards)]
    return mine, flipped, z, others


def greet(bits, shards, flipped, others):
    barrier = pltpu.get_barrier_semaphore()
    for b in range(bits):
        pl.semaphore_signal(
            barrier, inc=1, device_id={"rep": flipped[b]}, device_id_type=pl.DeviceIdType.MESH
        )
    for d in range(1, shards):
        pl.semaphore_signal(
            barrier, inc=1, device_id={"shard": others[d]}, device_id_type=pl.DeviceIdType.MESH
        )
    pl.semaphore_wait(barrier, bits + shards - 1)


def remote(src, dst, send, recv, where):
    copy = pltpu.make_async_remote_copy(
        src_ref=src,
        dst_ref=dst,
        send_sem=send,
        recv_sem=recv,
        device_id=where,
        device_id_type=pl.DeviceIdType.MESH,
    )
    copy.start()
    return copy


def bit_index(bits, mine, free):
    return tuple(slice(None) if b in free else mine[b] for b in reversed(range(bits)))


def norm_forward(values, gain, shift):
    centre = jnp.mean(values, axis=-1, keepdims=True)
    centred = values - centre
    inv_std = lax.rsqrt(jnp.mean(centred * centred, axis=-1, keepdims=True) + 1e-06)
    normed = centred * inv_std
    return normed * gain + shift, normed, inv_std


def norm_backward(grad_out, normed, inv_std, gain):
    scaled = grad_out * gain
    return inv_std * (
        scaled
        - jnp.mean(scaled, axis=-1, keepdims=True)
        - normed * jnp.mean(scaled * normed, axis=-1, keepdims=True)
    )


def gelu_parts(values):
    normal_cdf = 0.5 * (1.0 + lax.erf(values * inverse_root_two))
    slope = normal_cdf + values * jnp.exp(-0.5 * values * values) * inverse_root_tau
    return values * normal_cdf, slope


def dot(a, b):
    return lax.dot_general(a, b, (((1,), (0,)), ((), ())), preferred_element_type=F32)


def dot_nt(a, b):
    return lax.dot_general(a, b, (((1,), (1,)), ((), ())), preferred_element_type=F32)


def dot_tn(a, b):
    return lax.dot_general(a, b, (((0,), (0,)), ((), ())), preferred_element_type=F32)


def column_sum(values):
    return jnp.sum(values, axis=0, keepdims=True)


def chunks(bits, unit, start, count):
    found = []
    row = start
    while row < start + count:
        number, inside = divmod(row, unit)
        length = min(unit - inside, start + count - row)
        index = tuple((number >> b) & 1 for b in reversed(range(bits + 1)))
        found.append((index, slice(inside, inside + length), row - start, length))
        row += length
    return found


class Gather:
    def __init__(self, bits, shards, place, own, full, sems):
        self.bits, self.shards, self.own, self.full = bits, shards, own, full
        self.mine, self.flipped, self.z, self.others = place
        self.local_sem, self.z_send, self.z_recv, self.send, self.recv = sems
        self.orders = bit_orders(bits)
        self.hops, self.copies = {}, {}

    def start(self):
        piece = bit_index(self.bits, self.mine, ())
        for d in range(1, self.shards):
            self.hops[d] = remote(
                self.own.at[piece],
                self.full.at[(self.z,) + piece],
                self.z_send.at[d],
                self.z_recv.at[d],
                {"shard": self.others[d]},
            )
        self.local = pltpu.make_async_copy(self.own, self.full.at[self.z], self.local_sem)
        self.local.start()

    def step(self, t):
        for d in range(1, self.shards):
            source = lax.rem(self.z - d + self.shards, self.shards)
            for half in range(2):
                if t > 0:
                    self.copies[t - 1, d, half].wait_recv()
                elif half == 0:
                    self.hops[d].wait_recv()
                order = self.orders[half]
                where = (source,) + bit_index(self.bits, self.mine, order[:t]) + (half,)
                self.copies[t, d, half] = remote(
                    self.full.at[where],
                    self.full.at[where],
                    self.send.at[t, d, half],
                    self.recv.at[t, d, half],
                    {"rep": self.flipped[order[t]]},
                )

    def finish(self):
        for d in range(1, self.shards):
            for half in range(2):
                self.copies[self.bits - 1, d, half].wait_recv()
        self.local.wait()

    def drain(self):
        for copy in list(self.hops.values()) + list(self.copies.values()):
            copy.wait_send()


class Reduce:
    def __init__(self, bits, shards, place, total, out, landing, z_land, sems):
        self.bits, self.shards, self.total, self.out = bits, shards, total, out
        self.mine, self.flipped, self.z, self.others = place
        self.landing, self.z_land = landing, z_land
        self.z_send, self.z_recv, self.rs_send, self.rs_recv, self.ag_send, self.ag_recv = sems
        self.orders = bit_orders(bits)
        self.copies, self.gathers, self.hops = {}, {}, {}

    def add(self, t, half):
        self.copies[t, half].wait_recv()
        free = self.orders[half][: self.bits - 1 - t]
        keep = (slice(None),) + bit_index(self.bits, self.mine, free) + (half,)
        land = self.landing[2 * t + half]
        self.total[keep] = (self.total[keep].astype(F32) + land[...].astype(F32)).astype(BF16)

    def step(self, t):
        for half in range(2):
            if t > 0:
                self.add(t - 1, half)
            bit = self.orders[half][self.bits - 1 - t]
            theirs = list(self.mine)
            theirs[bit] = 1 - self.mine[bit]
            free = self.orders[half][: self.bits - 1 - t]
            where = (slice(None),) + bit_index(self.bits, theirs, free) + (half,)
            self.copies[t, half] = remote(
                self.total.at[where],
                self.landing[2 * t + half],
                self.rs_send.at[t, half],
                self.rs_recv.at[t, half],
                {"rep": self.flipped[bit]},
            )

    def hop(self):
        for half in range(2):
            self.add(self.bits - 1, half)
        piece = bit_index(self.bits, self.mine, ())
        for d in range(1, self.shards):
            self.hops[d] = remote(
                self.total.at[(self.others[d],) + piece],
                self.z_land.at[d],
                self.z_send.at[d],
                self.z_recv.at[d],
                {"shard": self.others[d]},
            )

    def own(self):
        piece = bit_index(self.bits, self.mine, ())
        value = self.total[(self.z,) + piece].astype(F32)
        for d in range(1, self.shards):
            self.hops[d].wait_recv()
            value = value + self.z_land[d].astype(F32)
        self.out[piece] = value.astype(BF16)

    def spread(self, t):
        for half in range(2):
            if t > 0:
                self.gathers[t - 1, half].wait_recv()
            order = self.orders[half]
            where = bit_index(self.bits, self.mine, order[:t]) + (half,)
            self.gathers[t, half] = remote(
                self.out.at[where],
                self.out.at[where],
                self.ag_send.at[t, half],
                self.ag_recv.at[t, half],
                {"rep": self.flipped[order[t]]},
            )

    def finish(self):
        for half in range(2):
            self.gathers[self.bits - 1, half].wait_recv()
        for group in (self.copies, self.hops, self.gathers):
            for copy in group.values():
                copy.wait_send()


def group_rows(needed, replicas):
    unit = 32 * replicas
    return -(-needed // unit) * unit


def layer_kernel(bits, shards, factor, *refs):
    x_ref, cot_ref, vec_ref, wqkv_ref, wo_ref, w1_ref, w2_ref = refs[:7]
    out_ref, gtok_ref, owned_a, owned_f, vec_out, fc1_out = refs[7:13]
    refs = refs[:7] + refs[9:]
    (flat, xpad, cpad, wqkv, wo, w1, w2, h1s, mixs, h2s, acts, cots, gps, grs, gqs) = refs[11:26]
    (qs, ks, vs, resids, greds, probs, vacc, own_a, own_f, full_a, full_f) = refs[26:37]
    z_land_a, z_land_f, pack_sem = refs[37:40]
    rest = refs[40:]
    g_a, g_f = full_a, full_f
    landing_a, landing_f, sems = rest[: 2 * bits], rest[2 * bits : 4 * bits], rest[4 * bits :]

    width = x_ref.shape[1]
    rows = width // shards
    hidden = w2.shape[0]
    slabs = hidden // width
    deep = slabs * rows
    images = x_ref.shape[0] // SEQ
    padded = xpad.shape[0] // images
    unit_a, unit_f = own_a.shape[-2], own_f.shape[-2]

    place = partners(bits, shards)
    greet(bits, shards, place[1], place[3])

    def pack(own, unit, sources, first):
        started = []
        for source, column, start, count in sources:
            for index, inside, offset, length in chunks(bits, unit, start, count):
                copy = pltpu.make_async_copy(
                    source.at[offset : offset + length, column : column + width],
                    own.at[index + (inside,)],
                    pack_sem.at[first + len(started)],
                )
                copy.start()
                started.append(copy)
        return started

    sources_a = [(wqkv_ref, c * width, c * rows, rows) for c in range(3)]
    sources_a += [(wo_ref, 0, 3 * rows, rows), (vec_ref, 0, 4 * rows, VEC_ROWS)]
    sources_f = [(w1_ref, j * width, j * rows, rows) for j in range(slabs)]
    sources_f += [(w2_ref, 0, deep, deep)]
    packs_a = pack(own_a, unit_a, sources_a, 0)
    packs_f = pack(own_f, unit_f, sources_f, len(packs_a))
    gather_a = Gather(bits, shards, place, own_a, full_a, sems[:5])
    gather_f = Gather(bits, shards, place, own_f, full_f, sems[5:10])
    for copy in packs_a:
        copy.wait()
    gather_a.start()
    for copy in packs_f:
        copy.wait()

    vacc[...] = jnp.zeros_like(vacc)
    for source, target in ((x_ref, xpad), (cot_ref, cpad)):
        target[...] = jnp.zeros_like(target)
        flat[...] = source[...].astype(F32)
        for i in range(images):
            target[i * padded : i * padded + SEQ, :] = flat[i * SEQ : (i + 1) * SEQ, :]
    gather_a.step(0)
    gather_f.start()
    for t in range(1, bits):
        gather_a.step(t)
    gather_a.finish()

    def unpack(full, unit, pairs):
        for target, row, column, start, count in pairs:
            for z in range(shards):
                for index, inside, offset, length in chunks(bits, unit, start, count):
                    at = row(z) + offset
                    target[at : at + length, column : column + width] = full[(z,) + index + (inside,)]

    thin = lambda z: z * rows
    thick = lambda z: z * deep
    unpack(full_a, unit_a, [(wqkv, thin, c * width, c * rows, rows) for c in range(3)])
    unpack(full_a, unit_a, [(wo, thin, 0, 3 * rows, rows)])

    def vec_of(z):
        index, inside, _, _ = chunks(bits, unit_a, 4 * rows, VEC_ROWS)[0]
        return full_a[(z,) + index + (inside,)].astype(F32)

    vec = vec_of(0)
    for z in range(1, shards):
        vec = vec + vec_of(z)
    gain_one, shift_one, q_shift, v_shift = (vec[r : r + 1, :] for r in range(4))
    out_shift, gain_two, shift_two, fc2_shift = (vec[r : r + 1, :] for r in range(4, 8))

    def rows_of(i):
        return pl.ds(pl.multiple_of(i * padded, 16), padded)

    def attend(i, carry):
        here = rows_of(i)
        x_float = xpad[here, :]
        norm_one, _, _ = norm_forward(x_float, gain_one, shift_one)
        hidden_one = norm_one.astype(BF16)
        h1s[here, :] = hidden_one
        query = (dot(hidden_one, wqkv[:, :width]) + q_shift).astype(BF16)
        keys = dot(hidden_one, wqkv[:, width : 2 * width]).astype(BF16)
        vals = (dot(hidden_one, wqkv[:, 2 * width :]) + v_shift).astype(BF16)
        qs[here, :] = query
        ks[here, :] = keys
        vs[here, :] = vals
        outside = lax.broadcasted_iota(jnp.int32, (padded, padded), 1) >= SEQ
        pieces = []
        for h in range(HEADS):
            cols = slice(h * HEAD_DIM, (h + 1) * HEAD_DIM)
            scores = dot_nt(query[:, cols], keys[:, cols]) * float(HEAD_DIM) ** (-0.5)
            scores = jnp.where(outside, -1e30, scores)
            top = jnp.max(scores, axis=-1, keepdims=True)
            grown = jnp.exp(scores - top)
            prob = grown * (1.0 / jnp.sum(grown, axis=-1, keepdims=True))
            probs[i, h] = prob
            pieces.append(dot(prob.astype(BF16), vals[:, cols]).astype(BF16))
        mixed = jnp.concatenate(pieces, axis=1)
        mixs[here, :] = mixed
        resids[here, :] = x_float + dot(mixed, wo[...]) + out_shift
        return carry

    gather_f.step(0)
    early, late = images // 4, images - images // 4
    lax.fori_loop(0, early, attend, 0)
    for t in range(1, bits - 1):
        gather_f.step(t)
    lax.fori_loop(early, late, attend, 0)
    gather_f.step(bits - 1)
    lax.fori_loop(late, images, attend, 0)
    gather_f.finish()
    unpack(full_f, unit_f, [(w1, thin, j * width, j * rows, rows) for j in range(slabs)])
    for z in range(shards):
        for index, inside, offset, length in chunks(bits, unit_f, deep, deep):
            at = z * deep + offset
            w2[at : at + length, :] = full_f[(z,) + index + (inside,)]

    def feed(i, carry):
        here = rows_of(i)
        resid = resids[here, :]
        cot_float = cpad[here, :]
        cot_b = cot_float.astype(BF16)
        cots[here, :] = cot_b
        norm_two, normed_two, inv_two = norm_forward(resid, gain_two, shift_two)
        hidden_two = norm_two.astype(BF16)
        h2s[here, :] = hidden_two
        total = resid + fc2_shift
        grad_h2 = jnp.zeros_like(resid)
        for j in range(slabs):
            cols = slice(j * width, (j + 1) * width)
            pre = dot(hidden_two, w1[:, cols]) + vec[8 + j : 9 + j, :]
            act, slope = gelu_parts(pre)
            act_b = act.astype(BF16)
            acts[here, cols] = act_b
            total = total + dot(act_b, w2[cols, :])
            grad_pre = dot_nt(cot_b, w2[cols, :]) * slope
            grad_pre_b = grad_pre.astype(BF16)
            gps[here, cols] = grad_pre_b
            vacc[8 + j : 9 + j, :] += column_sum(grad_pre)
            grad_h2 = grad_h2 + dot_nt(grad_pre_b, w1[:, cols])
        grad_resid = cot_float + norm_backward(grad_h2, normed_two, inv_two, gain_two)
        vacc[5:6, :] += column_sum(grad_h2 * normed_two)
        vacc[6:7, :] += column_sum(grad_h2)
        vacc[7:8, :] += column_sum(cot_float)
        vacc[4:5, :] += column_sum(grad_resid)
        cpad[here, :] = total
        greds[here, :] = grad_resid
        grs[here, :] = grad_resid.astype(BF16)
        return carry

    lax.fori_loop(0, images, feed, 0)

    def put(packed, unit, grad, per, start, count):
        for z in range(shards):
            for index, inside, offset, length in chunks(bits, unit, start, count):
                at = z * per + offset
                packed[(z,) + index + (inside,)] = grad[at : at + length].astype(BF16)

    gather_f.drain()
    for j in range(slabs):
        put(g_f, unit_f, dot_tn(h2s[...], gps[:, j * width : (j + 1) * width]), rows, j * rows, rows)
    for z in range(shards):
        grad = dot_tn(acts[:, z * deep : (z + 1) * deep], cots[...])
        for index, inside, offset, length in chunks(bits, unit_f, deep, deep):
            g_f[(z,) + index + (inside,)] = grad[offset : offset + length].astype(BF16)

    def blank(packed, unit, start):
        count = unit * 2 ** (bits + 1) - start
        for index, inside, _, length in chunks(bits, unit, start, count):
            for z in range(shards):
                packed[(z,) + index + (inside,)] = jnp.zeros((length, width), BF16)

    blank(g_f, unit_f, 2 * deep)
    reduce_f = Reduce(bits, shards, place, g_f, owned_f, landing_f, z_land_f, sems[10:16])
    reduce_a = Reduce(bits, shards, place, g_a, owned_a, landing_a, z_land_a, sems[16:22])
    reduce_f.step(0)

    def attend_back(i, carry):
        here = rows_of(i)
        grad_resid = greds[here, :]
        query, keys, vals = qs[here, :], ks[here, :], vs[here, :]
        grad_mixed = dot_nt(grs[here, :], wo[...]).astype(BF16)
        dq, dk, dv = [], [], []
        for h in range(HEADS):
            cols = slice(h * HEAD_DIM, (h + 1) * HEAD_DIM)
            prob = probs[i, h]
            grad_head = grad_mixed[:, cols]
            dv.append(dot_tn(prob.astype(BF16), grad_head))
            grad_prob = dot_nt(grad_head, vals[:, cols])
            inner = jnp.sum(prob * grad_prob, axis=-1, keepdims=True)
            grad_scores = (prob * (grad_prob - inner) * float(HEAD_DIM) ** (-0.5)).astype(BF16)
            dq.append(dot(grad_scores, keys[:, cols]))
            dk.append(dot_tn(grad_scores, query[:, cols]))
        grad_h1 = jnp.zeros_like(grad_resid)
        for c, parts in enumerate((dq, dk, dv)):
            grad = jnp.concatenate(parts, axis=1)
            if c == 0:
                vacc[2:3, :] += column_sum(grad)
            if c == 2:
                vacc[3:4, :] += column_sum(grad)
            grad_b = grad.astype(BF16)
            cols = slice(c * width, (c + 1) * width)
            gqs[here, cols] = grad_b
            grad_h1 = grad_h1 + dot_nt(grad_b, wqkv[:, cols])
        _, normed_one, inv_one = norm_forward(xpad[here, :], gain_one, shift_one)
        vacc[0:1, :] += column_sum(grad_h1 * normed_one)
        vacc[1:2, :] += column_sum(grad_h1)
        xpad[here, :] = grad_resid + norm_backward(grad_h1, normed_one, inv_one, gain_one)
        return carry

    lax.fori_loop(0, early, attend_back, 0)
    reduce_f.step(1)
    lax.fori_loop(early, late, attend_back, 0)
    for t in range(2, bits):
        reduce_f.step(t)
    lax.fori_loop(late, images, attend_back, 0)
    reduce_f.hop()
    gather_a.drain()
    for c in range(3):
        put(g_a, unit_a, dot_tn(h1s[...], gqs[:, c * width : (c + 1) * width]), rows, c * rows, rows)
    put(g_a, unit_a, dot_tn(mixs[...], grs[...]), rows, 3 * rows, rows)
    blank(g_a, unit_a, 4 * rows + VEC_ROWS)
    index, inside, _, _ = chunks(bits, unit_a, 4 * rows, VEC_ROWS)[0]
    for z in range(shards):
        g_a[(z,) + index + (inside,)] = vacc[...].astype(BF16)
    reduce_a.step(0)
    reduce_f.own()
    reduce_f.spread(0)
    for t in range(1, bits):
        reduce_a.step(t)
    for source, target in ((xpad, gtok_ref), (cpad, out_ref)):
        for i in range(images):
            flat[i * SEQ : (i + 1) * SEQ, :] = source[i * padded : i * padded + SEQ, :]
        target[...] = flat[...].astype(BF16)
    reduce_a.hop()
    for t in range(1, bits):
        reduce_f.spread(t)
    reduce_a.own()
    for t in range(bits):
        reduce_a.spread(t)
    reduce_f.finish()
    reduce_a.finish()
    sums = owned_a[index + (inside,)].astype(F32) * factor
    here = [(place[2] == z).astype(F32) for z in range(shards)]
    vec_out[...] = sum(here[z] * sums[:8, z * rows : (z + 1) * rows] for z in range(shards))
    fc1_out[...] = sum(here[z] * sums[8 + z : 9 + z, :] for z in range(shards))


def layer(tokens, cotangent, vec, w_qkv, w_out, w_fc1, w_fc2, bits, shards, factor):
    count, width = tokens.shape
    replicas = 2**bits
    rows = w_out.shape[0]
    hidden = w_fc1.shape[1]
    images = count // SEQ
    padded = -(-SEQ // 16) * 16
    long = images * padded
    rows_a = group_rows(4 * rows + VEC_ROWS, replicas)
    rows_f = group_rows(2 * rows * (hidden // width), replicas)
    twos = (2,) * bits
    tail_a = (rows_a // (2 * replicas), width)
    tail_f = (rows_f // (2 * replicas), width)
    full_a = (shards,) + twos + (2,) + tail_a
    full_f = (shards,) + twos + (2,) + tail_f

    def landing(tail):
        return [
            pltpu.VMEM((shards,) + (2,) * (bits - 1 - t) + tail, BF16)
            for t in range(bits)
            for _ in range(2)
        ]

    dma = pltpu.SemaphoreType.DMA
    gather_sems = [dma, dma((shards,)), dma((shards,)), dma((bits, shards, 2)), dma((bits, shards, 2))]
    reduce_sems = [dma((shards,)), dma((shards,))] + [dma((bits, 2))] * 4
    pieces = 0
    for unit, spans in (
        (tail_a[0], [(c * rows, rows) for c in range(4)] + [(4 * rows, VEC_ROWS)]),
        (tail_f[0], [(j * rows, rows) for j in range(hidden // width)] + [(rows_f0(rows, hidden, width),) * 2]),
    ):
        for start, length in spans:
            pieces += len(chunks(bits, unit, start, length))
    vmem = pl.BlockSpec(memory_space=pltpu.VMEM)
    left = pl.BlockSpec(memory_space=pl.ANY)
    return pl.pallas_call(
        functools.partial(layer_kernel, bits, shards, factor),
        out_shape=(
            jax.ShapeDtypeStruct(tokens.shape, BF16),
            jax.ShapeDtypeStruct(tokens.shape, BF16),
            jax.ShapeDtypeStruct(full_a[1:], BF16),
            jax.ShapeDtypeStruct(full_f[1:], BF16),
            jax.ShapeDtypeStruct((8, rows), F32),
            jax.ShapeDtypeStruct((1, width), F32),
        ),
        in_specs=[vmem] * 2 + [left] * 5,
        out_specs=(vmem,) * 6,
        scratch_shapes=[
            pltpu.VMEM((count, width), F32),
            pltpu.VMEM((long, width), F32),
            pltpu.VMEM((long, width), F32),
            pltpu.VMEM((width, 3 * width), BF16),
            pltpu.VMEM((width, width), BF16),
            pltpu.VMEM((width, hidden), BF16),
            pltpu.VMEM((hidden, width), BF16),
            pltpu.VMEM((long, width), BF16),
            pltpu.VMEM((long, width), BF16),
            pltpu.VMEM((long, width), BF16),
            pltpu.VMEM((long, hidden), BF16),
            pltpu.VMEM((long, width), BF16),
            pltpu.VMEM((long, hidden), BF16),
            pltpu.VMEM((long, width), BF16),
            pltpu.VMEM((long, 3 * width), BF16),
            pltpu.VMEM((long, width), BF16),
            pltpu.VMEM((long, width), BF16),
            pltpu.VMEM((long, width), BF16),
            pltpu.VMEM((long, width), F32),
            pltpu.VMEM((long, width), F32),
            pltpu.VMEM((images, HEADS, padded, padded), F32),
            pltpu.VMEM((VEC_ROWS, width), F32),
            pltpu.VMEM(full_a[1:], BF16),
            pltpu.VMEM(full_f[1:], BF16),
            pltpu.VMEM(full_a, BF16),
            pltpu.VMEM(full_f, BF16),
            pltpu.VMEM((shards, 2) + tail_a, BF16),
            pltpu.VMEM((shards, 2) + tail_f, BF16),
            dma((pieces,)),
            *landing(tail_a),
            *landing(tail_f),
            *gather_sems,
            *gather_sems,
            *reduce_sems,
            *reduce_sems,
        ],
        compiler_params=pltpu.CompilerParams(
            collective_id=0, has_side_effects=True, vmem_limit_bytes=62 << 20
        ),
        name="layer",
    )(tokens, cotangent, vec, w_qkv, w_out, w_fc1, w_fc2)


def rows_f0(rows, hidden, width):
    return rows * (hidden // width)


def per_device(
    tokens,
    cotangent,
    ln1_gain,
    ln1_bias,
    w_qkv,
    bias_qv,
    w_out,
    bias_out,
    ln2_gain,
    ln2_bias,
    w_fc1,
    bias_fc1,
    w_fc2,
    bias_fc2,
):
    replicas, shards = lax.axis_size("rep"), lax.axis_size("shard")
    bits = replicas.bit_length() - 1
    factor = float(tokens.shape[0] * replicas * shards) ** (-0.5)
    rows, width = w_out.shape
    slabs = w_fc1.shape[1] // width
    z = lax.axis_index("shard")
    small = jnp.stack(
        [ln1_gain, ln1_bias, bias_qv[0], bias_qv[1], bias_out, ln2_gain, ln2_bias, bias_fc2]
    )
    spread = jnp.concatenate([jnp.tile(small, (1, shards)), jnp.tile(bias_fc1[None, :], (8, 1))])
    row = lax.broadcasted_iota(jnp.int32, spread.shape, 0)
    lane = lax.broadcasted_iota(jnp.int32, spread.shape, 1)
    kept = ((row < 8) & (lane // rows == z)) | (row == 8 + z)
    vec = jnp.where(kept, spread, jnp.zeros_like(spread))
    layer_out, grad_tok, owned_a, owned_f, vectors, fc1_shift = layer(
        tokens, cotangent, vec, w_qkv, w_out, w_fc1, w_fc2, bits, shards, factor
    )
    owned_a = owned_a.reshape(-1, width)
    owned_f = owned_f.reshape(-1, width)

    def slab(owned, j):
        return owned[j * rows : (j + 1) * rows, :]

    def scale(value):
        return value.astype(F32) * factor

    return (
        layer_out,
        grad_tok,
        vectors[0],
        vectors[1],
        scale(jnp.concatenate([slab(owned_a, c) for c in range(3)], axis=1)),
        vectors[2:4],
        scale(slab(owned_a, 3)),
        vectors[4],
        vectors[5],
        vectors[6],
        scale(jnp.concatenate([slab(owned_f, j) for j in range(slabs)], axis=1)),
        fc1_shift[0],
        scale(owned_f[slabs * rows : 2 * slabs * rows, :]),
        vectors[7],
    )


def solution(mesh):
    both = P(("rep", "shard"), None)
    lone = P("shard")
    flat = P("shard", None)
    pair = P(None, "shard")
    params = (lone, lone, flat, pair, flat, lone, lone, lone, flat, lone, flat, lone)
    return jax.shard_map(
        per_device,
        mesh=mesh,
        in_specs=(both, both) + params,
        out_specs=(both, both) + params,
        check_vma=False,
    )
```
